1024 devices in a mesh: ctx: 128 (over y, z), chan: 8 (over x, core).
Axes of the slice: x: 4, y: 4, z: 32, core: 2. Of those that a mesh axis runs over, the one named last changes fastest.
Arguments:
- features: bfloat16 [32768, 3, 8192], P('ctx', None, 'chan'), may hold values from -29 to 29
- short_taps: float32 [3, 3, 8192], P(None, None, 'chan'), may hold values from -3 to 3
- decay_rate: float32 [16, 8192], P(None, 'chan'), may hold values from 1.5258789e-05 to 0.0333333333
- residue: float32 [16, 8192], P(None, 'chan'), may hold values from -1.5 to 1.5
- skip_gain: float32 [8192], P('chan'), may hold values from -4 to 4
- norm_gain: float32 [8192], P('chan'), may hold values from 0.5 to 1.5
- contig_lengths: int32 [4], replicated, may hold values from 1 to 16384, 32768 in all
Outputs:
- normed: bfloat16 [32768, 8192], P('ctx', 'chan')
The draws below stay inside these ranges and needn't reach their ends.
Inputs may be any that keep to these rules, and one draw needn't show every extreme that they name: `contig_lengths`: the lengths sum to 32768 and the longest is exactly 16384.
All inputs are finite; a program needn't handle non-finite values.
Results may differ from the reference program's by a relative error of at most 0.0024.
Values may be sent and summed in bfloat16 or wider, within the bound.
No kernel may reach another device: no remote copies, remote signals or barrier semaphores. Data moves between devices by JAX's collectives and lax.ppermute only.
A program may use at most 64 MiB of HBM per device.

```python
import math
import jax
import jax.numpy as jnp
import numpy as np
from jax import lax

D = 8192
ORDER = 16
NCONTIG = 4
TOKENS = 32768


def draw_features(key, part):
    key_one = jax.random.fold_in(jax.random.fold_in(key, 11), 0)
    columns = 3.0 ** (jnp.arange(D, dtype=jnp.float32) / (3.0 * D))
    values = jnp.clip(jax.random.normal(key_one, (TOKENS, 3, D), jnp.float32), -5.0, 5.0) * columns
    return values.astype(jnp.bfloat16)


def draw_decay_rate(key, part):
    key_one, key_two, key_three, key_four, key_five = jax.random.split(jax.random.fold_in(key, 23), 5)
    low_end = math.log(0.5 / TOKENS)
    mid_end = math.log(min(4.0 / TOKENS, 1.0 / 64.0))
    top_end = math.log(1.0 / 64.0)
    very_slow = jnp.exp(low_end + jax.random.uniform(key_one, (ORDER, D), jnp.float32) * (mid_end - low_end))
    middle = jnp.exp(mid_end + jax.random.uniform(key_four, (ORDER, D), jnp.float32) * (top_end - mid_end))
    slow_rate = jnp.where(jax.random.uniform(key_five, (ORDER, D), jnp.float32) < 0.5, very_slow, middle)
    fast_rate = jnp.exp(math.log(1.0 / 50.0) + jax.random.uniform(key_three, (ORDER, D), jnp.float32) * math.log(50.0 / 30.0))
    share = 0.5
    picked = jax.random.uniform(key_two, (ORDER, D), jnp.float32)
    return jnp.where(picked < share, slow_rate, fast_rate).astype(jnp.float32)


def shard_levels(rng, dims, cuts, low, largest):
    def one(position, blocks):
        steps = jax.random.uniform(jax.random.fold_in(jax.random.fold_in(rng, 6), position), (blocks,), jnp.float32, low / len(cuts), largest / len(cuts))
        return jnp.repeat(jnp.exp(steps), dims[position] // blocks).reshape((-1,) + (1,) * (len(dims) - position - 1))

    level = one(*cuts[0])
    for cut in cuts[1:]:
        level = level * one(*cut)
    return level


def length_profile(count, total, bound, lean):
    loads = [(1 << 20) // math.isqrt(grade ** lean) + 1 for grade in range(2, count + 1)]
    spare, counts = total - bound - (count - 1), [1] * (count - 1)
    while spare > 0:
        candidates = [i for i in range(count - 1) if counts[i] < bound]
        whole, left = sum([loads[i] for i in candidates]), spare
        for i in candidates:
            addition = min(bound - counts[i], max(1, left * loads[i] // whole), spare)
            counts[i] = counts[i] + addition
            spare = spare - addition
    return np.array([bound] + counts)


def uneven_parts(own_key, amount, total, most, slope):
    if amount == 2:
        one = jax.random.randint(own_key, (), max(1, total - most), min(most, total - 1) + 1)
        return jnp.stack([one, total - one])
    sizes = jnp.asarray(length_profile(amount, total, most, slope), jnp.int32)
    couples = (amount - 1) // 2
    donor, taker = sizes[1:1 + 2 * couples:2], sizes[2:2 + 2 * couples:2]
    margin = jnp.minimum(donor - 1, most - taker)
    shifted = jax.random.randint(jax.random.fold_in(own_key, 1), (couples,), 0, 1 << 20) % (margin + 1)
    sizes = sizes.at[1:1 + 2 * couples:2].set(donor - shifted).at[2:2 + 2 * couples:2].set(taker + shifted)
    return sizes[jax.random.permutation(jax.random.fold_in(own_key, 2), amount)]


def scatter_about(own_key, dims, spread, reach, cuts=(), kind=jnp.bfloat16):
    factor_of = shard_levels(own_key, dims, cuts, -0.22, 0.18) if cuts else 1.0
    entries = jax.random.normal(own_key, dims, jnp.float32) * spread * factor_of
    return jnp.minimum(jnp.maximum(entries, -reach), reach).astype(kind)


def setup_inputs(seed: int = 0) -> dict:
    keys = jax.random.split(jax.random.key(seed), 8)
    return {
        "features": draw_features(jax.random.fold_in(keys[7], 71), 0),
        "short_taps": scatter_about(keys[1], (3, 3, D), 0.6, 3.0, ((2, 8),), jnp.float32),
        "decay_rate": draw_decay_rate(jax.random.fold_in(keys[7], 71), 0),
        "residue": scatter_about(keys[3], (ORDER, D), 0.25, 1.5, ((1, 8),), jnp.float32),
        "skip_gain": scatter_about(keys[4], (D,), 1.0, 4.0, ((0, 8),), jnp.float32),
        "norm_gain": jnp.clip(1.0 + 0.1 * jax.random.normal(keys[5], (D,), jnp.float32), 0.5, 1.5),
        "contig_lengths": uneven_parts(keys[6], NCONTIG, TOKENS, TOKENS // 2, 1).astype(jnp.int32),
    }


eps_norm = 1e-05

def reference(features, short_taps, decay_rate, residue, skip_gain, norm_gain, contig_lengths):
    bounds = jnp.cumsum(contig_lengths)[:-1]
    places = jnp.arange(TOKENS, dtype=jnp.int32)
    segment = lax.optimization_barrier(jnp.sum((places[:, None] >= bounds[None, :]).astype(jnp.int32), axis=1))
    keep_one = jnp.concatenate([jnp.zeros((1,), jnp.float32), (segment[1:] == segment[:-1]).astype(jnp.float32)])
    keep_two = jnp.concatenate([jnp.zeros((2,), jnp.float32), (segment[2:] == segment[:-2]).astype(jnp.float32)])
    fade = jnp.exp(-decay_rate)
    input_scale = jnp.sqrt(1.0 - jnp.exp(-2.0 * decay_rate))

    def advance(carry, inputs):
        state, prev_one, prev_two = carry
        row_now, link_one, link_two = inputs
        current = row_now.astype(jnp.float32)
        mixed_rows = short_taps[0] * current + short_taps[1] * prev_one * link_one + short_taps[2] * prev_two * link_two
        product = mixed_rows[1] * mixed_rows[2]
        state = fade * state * link_one + input_scale * product[None, :]
        filtered = lax.optimization_barrier(jnp.sum(residue * state, axis=0))
        response = mixed_rows[0] * (filtered + skip_gain * product)
        scale_row = lax.rsqrt(jnp.mean(response * response) + eps_norm)
        return ((state, current, prev_one), (response * scale_row * norm_gain).astype(jnp.bfloat16))
    start = (jnp.zeros((ORDER, D), jnp.float32), jnp.zeros((3, D), jnp.float32), jnp.zeros((3, D), jnp.float32))
    final_carry, normed = lax.scan(advance, start, (features, keep_one, keep_two), unroll=8)
    return normed
```

```python
import functools

import jax
import jax.numpy as jnp
from jax import lax
from jax.experimental import pallas as pl
from jax.experimental.pallas import tpu as pltpu
from jax.sharding import PartitionSpec as P

D = 8192
eps_norm = 1e-05
CHUNK = 16
PAD = 8
HIGH = lax.Precision.HIGHEST


def starts_of(lengths, anchor):
    one = lengths[0]
    two = one + lengths[1]
    three = two + lengths[2]
    return [-anchor, one - anchor, two - anchor, three - anchor]


def hits(starts, low, high):
    found = (starts[0] >= low) & (starts[0] < high)
    for start in starts[1:]:
        found = found | ((start >= low) & (start < high))
    return found


def as_tiles(rows, ref, sub, lanes):
    for tile in range(sub):
        rows[pl.ds(tile * ref.shape[0], ref.shape[0]), :] = ref[:, tile * lanes : (tile + 1) * lanes]


def row_tile(rows, row, count, sub):
    return rows[pl.ds(row, sub, stride=count), :]


def first_pass(lengths, x_ref, edge_ref, taps_ref, rate_ref, state_ref, product_ref, query_ref,
               spread, rate_rows, taps_rows):
    toks, sub, lanes = product_ref.shape
    poles = rate_ref.shape[0]
    pitch = toks + PAD
    anchor = lax.axis_index("ctx") * toks
    starts = starts_of(lengths, anchor)
    for part in range(3):
        for tile in range(sub):
            cols = slice(tile * lanes, (tile + 1) * lanes)
            spread[part, pl.ds(tile * pitch + PAD, toks), :] = x_ref[part, :, cols].astype(jnp.float32)
            spread[part, pl.ds(tile * pitch + PAD - 2, 2), :] = edge_ref[part, :, cols].astype(jnp.float32)
    as_tiles(rate_rows, rate_ref, sub, lanes)
    for tap in range(3):
        for part in range(3):
            for tile in range(sub):
                taps_rows[tap * 3 + part, pl.ds(tile, 1), :] = taps_ref[
                    tap, pl.ds(part, 1), tile * lanes : (tile + 1) * lanes
                ]
    fades = [jnp.exp(-row_tile(rate_rows, n, poles, sub)) for n in range(poles)]
    state_ref[...] = jnp.zeros_like(state_ref)

    def token_rows(t):
        return [spread[part, pl.ds(t + PAD, sub, stride=pitch), :] for part in range(3)]

    def chunk(index, _):
        base = index * CHUNK

        def steps(masked):
            states = [state_ref[n] for n in range(poles)]
            two, one = token_rows(base - 2), token_rows(base - 1)
            for i in range(CHUNK):
                t = base + i
                now = token_rows(t)
                if masked:
                    link_one = jnp.where(hits(starts, t, t + 1), 0.0, 1.0).astype(jnp.float32)
                    link_two = jnp.where(hits(starts, t - 1, t + 1), 0.0, 1.0).astype(jnp.float32)
                mixed = []
                for part in range(3):
                    term_one = taps_rows[3 + part] * one[part]
                    term_two = taps_rows[6 + part] * two[part]
                    if masked:
                        term_one, term_two = term_one * link_one, term_two * link_two
                    mixed.append(taps_rows[part] * now[part] + term_one + term_two)
                product = mixed[1] * mixed[2]
                query_ref[t] = mixed[0]
                product_ref[t] = product
                if masked:
                    states = [s * link_one for s in states]
                states = [fades[n] * states[n] + product for n in range(poles)]
                two, one = one, now
            for n in range(poles):
                state_ref[n] = states[n]

        cut = hits(starts, base - 1, base + CHUNK)

        @pl.when(cut)
        def _():
            steps(True)

        @pl.when(jnp.logical_not(cut))
        def _():
            steps(False)

        return 0

    lax.fori_loop(0, toks // CHUNK, chunk, 0)


def scan_devices(toks, lengths, ends_ref, rate_ref, arrived_ref, rows):
    count, lanes = ends_ref.shape
    sub = rate_ref.shape[1] // lanes
    mine = lax.axis_index("ctx")
    as_tiles(rows, rate_ref, sub, lanes)
    rate = rows[pl.ds((mine % sub) * rate_ref.shape[0] + mine // sub, 1), :]
    place = lax.broadcasted_iota(jnp.int32, (count, lanes), 0)
    first = place * toks
    cut = hits(starts_of(lengths, 0), first, first + toks)
    factor = jnp.where(cut, 0.0, jnp.exp(rate * (-float(toks))))
    total = ends_ref[...]
    step = 1
    while step < count:
        total = total + factor * pltpu.roll(total, step, 0)
        factor = factor * pltpu.roll(factor, step, 0)
        step *= 2
    arrived_ref[...] = jnp.where(place == 0, 0.0, pltpu.roll(total, 1, 0))


def second_pass(lengths, arrived_ref, product_ref, query_ref, rate_ref, residue_ref, skip_ref,
                response_ref, squares_ref, spread, states_ref, rate_rows, residue_rows):
    toks, sub, lanes = product_ref.shape
    poles = rate_ref.shape[0]
    anchor = lax.axis_index("ctx") * toks
    starts = starts_of(lengths, anchor)
    as_tiles(rate_rows, rate_ref, sub, lanes)
    as_tiles(residue_rows, residue_ref, sub, lanes)
    fades, gains = [], []
    for n in range(poles):
        rate = row_tile(rate_rows, n, poles, sub)
        fades.append(jnp.exp(-rate))
        gains.append(row_tile(residue_rows, n, poles, sub) * jnp.sqrt(1.0 - jnp.exp(-2.0 * rate)))
    skip = skip_ref[...]
    states_ref[...] = arrived_ref[...]

    def chunk(index, _):
        base = index * CHUNK

        def steps(masked):
            states = [states_ref[n] for n in range(poles)]
            for i in range(CHUNK):
                t = base + i
                product = product_ref[t]
                if masked:
                    link = jnp.where(hits(starts, t, t + 1), 0.0, 1.0).astype(jnp.float32)
                    states = [s * link for s in states]
                states = [fades[n] * states[n] + product for n in range(poles)]
                sums = [gains[n] * states[n] for n in range(poles)] + [skip * product]
                while len(sums) > 1:
                    sums = [a + b for a, b in zip(sums[::2], sums[1::2])] + (
                        [sums[-1]] if len(sums) % 2 else []
                    )
                spread[pl.ds(t, sub, stride=toks), :] = query_ref[t] * sums[0]
            for n in range(poles):
                states_ref[n] = states[n]

        cut = hits(starts, base, base + CHUNK)

        @pl.when(cut)
        def _():
            steps(True)

        @pl.when(jnp.logical_not(cut))
        def _():
            steps(False)

        return 0

    lax.fori_loop(0, toks // CHUNK, chunk, 0)
    total = jnp.zeros((toks, lanes), jnp.float32)
    for tile in range(sub):
        part = spread[pl.ds(tile * toks, toks), :]
        response_ref[:, tile * lanes : (tile + 1) * lanes] = part
        total = total + part * part
    sums = lax.dot_general(
        jnp.ones((squares_ref.shape[0], lanes), jnp.float32), total, (((1,), (1,)), ((), ())),
        precision=HIGH, preferred_element_type=jnp.float32,
    )
    halves = toks // lanes
    half = lax.broadcasted_iota(jnp.int32, squares_ref.shape, 0) % halves
    picked = sums[:, :lanes]
    for h in range(1, halves):
        picked = jnp.where(half == h, sums[:, h * lanes : (h + 1) * lanes], picked)
    squares_ref[...] = picked


def last_pass(squares_ref, response_ref, gain_ref, out_ref):
    count, lanes = squares_ref.shape
    halves = out_ref.shape[0] // lanes
    half = lax.broadcasted_iota(jnp.int32, (count, lanes), 0) % halves
    for h in range(halves):
        sums = lax.dot_general(
            squares_ref[...], (half == h).astype(jnp.float32), (((0,), (0,)), ((), ())),
            precision=HIGH, preferred_element_type=jnp.float32,
        )
        scale = lax.rsqrt(sums / D + eps_norm)
        toks = slice(h * lanes, (h + 1) * lanes)
        for tile in range(response_ref.shape[1] // lanes):
            cols = slice(tile * lanes, (tile + 1) * lanes)
            out_ref[toks, cols] = (response_ref[toks, cols] * scale * gain_ref[:, cols]).astype(jnp.bfloat16)


SCALARS = pl.BlockSpec(memory_space=pltpu.SMEM)
VECTORS = pl.BlockSpec(memory_space=pltpu.VMEM)
F32 = jnp.float32


def call(body, inputs, outputs, scratch, name):
    return pl.pallas_call(
        body,
        in_specs=[SCALARS if i is None else VECTORS for i in inputs],
        out_specs=jax.tree.map(lambda _: VECTORS, outputs),
        out_shape=outputs,
        scratch_shapes=scratch,
        compiler_params=pltpu.CompilerParams(vmem_limit_bytes=40 << 20),
        name=name,
    )


def shards(features, short_taps, decay_rate, residue, skip_gain, norm_gain, contig_lengths):
    toks, _, channels = features.shape
    poles = decay_rate.shape[0]
    lanes, sub = 128, channels // 128
    count, wide = lax.axis_size("ctx"), lax.axis_size("chan")
    tile = lambda *lead: jax.ShapeDtypeStruct((*lead, sub, lanes), F32)
    flat = lambda *dims: jax.ShapeDtypeStruct(dims, F32)
    rows = pltpu.VMEM((poles * sub, lanes), F32)
    parts = jnp.transpose(features, (1, 0, 2))
    edge = lax.ppermute(parts[:, toks - 2 :], "ctx", [(i, i + 1) for i in range(count - 1)])
    ends, product, query = call(
        first_pass, [None, 1, 1, 1, 1], (tile(poles), tile(toks), tile(toks)),
        [pltpu.VMEM((3, sub * (toks + PAD), lanes), F32), rows, pltpu.VMEM((9, sub, lanes), F32)],
        "first_pass",
    )(contig_lengths, parts, edge, short_taps, decay_rate)
    ends = lax.all_to_all(jnp.reshape(ends, (poles * sub, lanes)), "ctx", 0, 0, tiled=True)
    arrived = call(
        functools.partial(scan_devices, toks), [None, 1, 1], flat(count, lanes), [rows], "scan_devices"
    )(contig_lengths, ends, decay_rate)
    arrived = lax.all_to_all(arrived, "ctx", 0, 0, tiled=True)
    response, squares = call(
        second_pass, [None, 1, 1, 1, 1, 1, 1],
        (flat(toks, channels), flat(wide * toks // lanes, lanes)),
        [pltpu.VMEM((sub * toks, lanes), F32), pltpu.VMEM((poles, sub, lanes), F32), rows, rows],
        "second_pass",
    )(contig_lengths, jnp.reshape(arrived, (poles, sub, lanes)), product, query, decay_rate, residue,
      jnp.reshape(skip_gain, (sub, lanes)))
    squares = lax.all_to_all(squares, "chan", 0, 0, tiled=True)
    return call(
        last_pass, [1, 1, 1], jax.ShapeDtypeStruct((toks, channels), jnp.bfloat16), [], "last_pass"
    )(squares, response, jnp.reshape(norm_gain, (1, channels)))


def solution(mesh):
    placed = (
        P("ctx", None, "chan"),
        P(None, None, "chan"),
        P(None, "chan"),
        P(None, "chan"),
        P("chan"),
        P("chan"),
        P(),
    )
    return jax.shard_map(
        shards, mesh=mesh, in_specs=placed, out_specs=P("ctx", "chan"), check_vma=False
    )
```

```python
import functools

import jax
import jax.numpy as jnp
from jax import lax
from jax.experimental import pallas as pl
from jax.experimental.pallas import tpu as pltpu
from jax.sharding import Mesh, PartitionSpec as P

D = 8192
eps_norm = 1e-05
CHUNK = 16
PAD = 8
PIECES = 4
CTX = ("row", "far", "near")
HIGH = lax.Precision.HIGHEST


def starts_of(lengths, anchor):
    one = lengths[0]
    two = one + lengths[1]
    three = two + lengths[2]
    return [-anchor, one - anchor, two - anchor, three - anchor]


def hits(starts, low, high):
    found = (starts[0] >= low) & (starts[0] < high)
    for start in starts[1:]:
        found = found | ((start >= low) & (start < high))
    return found


def as_tiles(rows, ref, sub, lanes):
    for tile in range(sub):
        rows[pl.ds(tile * ref.shape[0], ref.shape[0]), :] = ref[:, tile * lanes : (tile + 1) * lanes]


def row_tile(rows, row, count, sub):
    return rows[pl.ds(row, sub, stride=count), :]


def mix(taps, now, one, two):
    return [taps[part] * now[part] + taps[3 + part] * one[part] + taps[6 + part] * two[part] for part in range(3)]


def scaled(rows, link):
    return [row * link for row in rows]


def link_at(starts, low, high):
    return jnp.where(hits(starts, low, high), 0.0, 1.0).astype(jnp.float32)


def first_pass(lengths_hbm, x_hbm, taps_hbm, rate_hbm, state_ref, product_ref, query_ref, consts_ref,
               lengths, held, spread, taps_held, rate_held, rate_rows, taps_rows, sems, x_sems):
    toks, sub, lanes = product_ref.shape
    poles = rate_held.shape[0]
    pitch = toks + PAD
    pieces = held.shape[0]
    span = toks // pieces
    small = [
        pltpu.make_async_copy(source, target, sems.at[i])
        for i, (source, target) in enumerate(
            [(lengths_hbm, lengths), (taps_hbm, taps_held), (rate_hbm, rate_held)]
        )
    ]
    for copy in small:
        copy.start()

    def piece_copy(piece):
        return pltpu.make_async_copy(
            x_hbm.at[:, pl.ds(pl.multiple_of(piece * span, span), span), :], held.at[piece], x_sems.at[piece]
        )

    for piece in range(pieces):
        piece_copy(piece).start()
    for copy in small:
        copy.wait()
    anchor = lax.axis_index(CTX) * toks
    starts = starts_of(lengths, anchor)
    as_tiles(rate_rows, rate_held, sub, lanes)
    for tap in range(3):
        for part in range(3):
            for tile in range(sub):
                taps_rows[tap * 3 + part, pl.ds(tile, 1), :] = taps_held[
                    tap, pl.ds(part, 1), tile * lanes : (tile + 1) * lanes
                ]
    fades = []
    for n in range(poles):
        rate = row_tile(rate_rows, n, poles, sub)
        consts_ref[n] = rate
        fades.append(jnp.exp(-rate))
    for row in range(9):
        consts_ref[poles + row] = taps_rows[row]
    state_ref[...] = jnp.zeros_like(state_ref)

    def token_rows(t):
        return [spread[part, pl.ds(t + PAD, sub, stride=pitch), :] for part in range(3)]

    def chunk(index, _):
        base = index * CHUNK

        def steps(masked):
            states = [state_ref[n] for n in range(poles)]
            two, one = token_rows(base - 2), token_rows(base - 1)
            for i in range(CHUNK):
                t = base + i
                now = token_rows(t)
                if masked:
                    link = link_at(starts, t, t + 1)
                    mixed = mix(taps_rows, now, scaled(one, link), scaled(two, link_at(starts, t - 1, t + 1)))
                    states = scaled(states, link)
                else:
                    mixed = mix(taps_rows, now, one, two)
                product = mixed[1] * mixed[2]
                query_ref[t] = mixed[0]
                product_ref[t] = product
                if masked and i < 2:
                    product = jnp.where(index == 0, 0.0, product)
                states = [fades[n] * states[n] + product for n in range(poles)]
                two, one = one, now
            for n in range(poles):
                state_ref[n] = states[n]

        cut = hits(starts, base - 1, base + CHUNK) | (index == 0)

        @pl.when(cut)
        def _():
            steps(True)

        @pl.when(jnp.logical_not(cut))
        def _():
            steps(False)

        return 0

    def piece_step(piece, _):
        piece_copy(piece).wait()
        for part in range(3):
            for tile in range(sub):
                row = pl.multiple_of(piece * span, span) + (tile * pitch + PAD)
                spread[part, pl.ds(pl.multiple_of(row, 8), span), :] = held[
                    piece, part, :, tile * lanes : (tile + 1) * lanes
                ].astype(jnp.float32)
        lax.fori_loop(piece * (span // CHUNK), (piece + 1) * (span // CHUNK), chunk, 0)
        return 0

    lax.fori_loop(0, pieces, piece_step, 0)
    for i in range(2):
        for part, row in enumerate(token_rows(i)):
            consts_ref[poles + 9 + i * 3 + part] = row


def edge_pass(toks, lengths, edge_ref, consts_ref, state_ref, ends_ref, head_ref, spread):
    poles, sub, lanes = state_ref.shape
    anchor = lax.axis_index(CTX) * toks
    starts = starts_of(lengths, anchor)
    for part in range(3):
        for tile in range(sub):
            spread[part, pl.ds(tile * 2, 2), :] = edge_ref[
                part, :, tile * lanes : (tile + 1) * lanes
            ].astype(jnp.float32)
    earlier = [[spread[part, pl.ds(i, sub, stride=2), :] for part in range(3)] for i in range(2)]
    heads = [[consts_ref[poles + 9 + i * 3 + part] for part in range(3)] for i in range(2)]
    taps = [consts_ref[poles + row] for row in range(9)]
    at_zero = mix(taps, heads[0], scaled(earlier[1], link_at(starts, 0, 1)), scaled(earlier[0], link_at(starts, -1, 1)))
    at_one = mix(taps, heads[1], scaled(heads[0], link_at(starts, 1, 2)), scaled(earlier[1], link_at(starts, 0, 2)))
    zero, one = at_zero[1] * at_zero[2], at_one[1] * at_one[2]
    head_ref[0], head_ref[1], head_ref[2], head_ref[3] = zero, one, at_zero[0], at_one[0]
    zero, one = zero * link_at(starts, 1, toks), one * link_at(starts, 2, toks)
    for n in range(poles):
        rate = consts_ref[n]
        late = jnp.exp(rate * (-float(toks - 2)))
        ends_ref[n] = state_ref[n] + late * (jnp.exp(-rate) * zero + one)


def whole(starts, first, count):
    return link_at(starts, first, first + count)


def block_totals(toks, lengths, ends_ref, consts_ref, totals_ref):
    rows, near = lax.axis_size("row"), lax.axis_size("near")
    far = lax.axis_size("far")
    keep = jnp.exp(consts_ref[lax.axis_index("row") * near + lax.axis_index("near")] * (-float(toks)))
    starts = starts_of(lengths, 0)
    for row in range(rows):
        first = (row * far + lax.axis_index("far")) * (near * toks)
        total = ends_ref[row * near]
        for i in range(1, near):
            total = ends_ref[row * near + i] + total * (keep * whole(starts, first + i * toks, toks))
        for g in range(far):
            totals_ref[g * rows + row] = total


def spread_carry(toks, lengths, ends_ref, totals_ref, consts_ref, arrived_ref):
    rows, near, far = lax.axis_size("row"), lax.axis_size("near"), lax.axis_size("far")
    mine = lax.axis_index("far")
    rate = consts_ref[lax.axis_index("row") * near + lax.axis_index("near")]
    span = near * toks
    keep, keep_span = jnp.exp(rate * (-float(toks))), jnp.exp(rate * (-float(span)))
    starts = starts_of(lengths, 0)
    carry = jnp.zeros_like(keep)
    for row in range(rows):
        mid = carry
        for g in range(far):
            mid = jnp.where(g == mine, carry, mid)
            carry = totals_ref[g * rows + row] + carry * (keep_span * whole(starts, (row * far + g) * span, span))
        first = (row * far + mine) * span
        for i in range(near):
            arrived_ref[row * near + i] = mid
            mid = ends_ref[row * near + i] + mid * (keep * whole(starts, first + i * toks, toks))


def second_pass(lengths, arrived_ref, head_ref, product_ref, query_ref, consts_ref, residue_ref, skip_ref,
                response_ref, squares_ref, spread, states_ref, residue_rows):
    toks, sub, lanes = product_ref.shape
    poles = residue_ref.shape[0]
    anchor = lax.axis_index(CTX) * toks
    starts = starts_of(lengths, anchor)
    as_tiles(residue_rows, residue_ref, sub, lanes)
    fades, gains = [], []
    for n in range(poles):
        rate = consts_ref[n]
        fades.append(jnp.exp(-rate))
        gains.append(row_tile(residue_rows, n, poles, sub) * jnp.sqrt(1.0 - jnp.exp(-2.0 * rate)))
    skip = skip_ref[...]
    states_ref[...] = arrived_ref[...]

    def chunk(index, _):
        base = index * CHUNK

        def steps(masked):
            states = [states_ref[n] for n in range(poles)]
            for i in range(CHUNK):
                t = base + i
                product, query = product_ref[t], query_ref[t]
                if masked:
                    states = scaled(states, link_at(starts, t, t + 1))
                    if i < 2:
                        product = jnp.where(index == 0, head_ref[i], product)
                        query = jnp.where(index == 0, head_ref[2 + i], query)
                states = [fades[n] * states[n] + product for n in range(poles)]
                sums = [gains[n] * states[n] for n in range(poles)] + [skip * product]
                while len(sums) > 1:
                    sums = [a + b for a, b in zip(sums[::2], sums[1::2])] + (
                        [sums[-1]] if len(sums) % 2 else []
                    )
                spread[pl.ds(t, sub, stride=toks), :] = query * sums[0]
            for n in range(poles):
                states_ref[n] = states[n]

        cut = hits(starts, base, base + CHUNK) | (index == 0)

        @pl.when(cut)
        def _():
            steps(True)

        @pl.when(jnp.logical_not(cut))
        def _():
            steps(False)

        return 0

    lax.fori_loop(0, toks // CHUNK, chunk, 0)
    total = jnp.zeros((toks, lanes), jnp.float32)
    for tile in range(sub):
        part = spread[pl.ds(tile * toks, toks), :]
        response_ref[:, tile * lanes : (tile + 1) * lanes] = part
        total = total + part * part
    sums = lax.dot_general(
        jnp.ones((squares_ref.shape[0], lanes), jnp.float32), total, (((1,), (1,)), ((), ())),
        precision=HIGH, preferred_element_type=jnp.float32,
    )
    halves = toks // lanes
    half = lax.broadcasted_iota(jnp.int32, squares_ref.shape, 0) % halves
    picked = sums[:, :lanes]
    for h in range(1, halves):
        picked = jnp.where(half == h, sums[:, h * lanes : (h + 1) * lanes], picked)
    squares_ref[...] = picked


def last_pass(squares_ref, response_ref, gain_ref, out_ref):
    count, lanes = squares_ref.shape
    halves = out_ref.shape[0] // lanes
    half = lax.broadcasted_iota(jnp.int32, (count, lanes), 0) % halves
    for h in range(halves):
        sums = lax.dot_general(
            squares_ref[...], (half == h).astype(jnp.float32), (((0,), (0,)), ((), ())),
            precision=HIGH, preferred_element_type=jnp.float32,
        )
        scale = lax.rsqrt(sums / D + eps_norm)
        toks = slice(h * lanes, (h + 1) * lanes)
        for tile in range(response_ref.shape[1] // lanes):
            cols = slice(tile * lanes, (tile + 1) * lanes)
            out_ref[toks, cols] = (response_ref[toks, cols] * scale * gain_ref[:, cols]).astype(jnp.bfloat16)


SCALARS = pl.BlockSpec(memory_space=pltpu.SMEM)
VECTORS = pl.BlockSpec(memory_space=pltpu.VMEM)
ANYWHERE = pl.BlockSpec(memory_space=pltpu.HBM)
F32 = jnp.float32
SPECS = {"s": SCALARS, "v": VECTORS, "a": ANYWHERE}


def call(body, inputs, outputs, scratch, name):
    return pl.pallas_call(
        body,
        in_specs=[SPECS[i] for i in inputs],
        out_specs=jax.tree.map(lambda _: VECTORS, outputs),
        out_shape=outputs,
        scratch_shapes=scratch,
        compiler_params=pltpu.CompilerParams(vmem_limit_bytes=40 << 20),
        name=name,
    )


def shards(features, short_taps, decay_rate, residue, skip_gain, norm_gain, contig_lengths):
    toks, _, channels = features.shape
    poles = decay_rate.shape[0]
    lanes, sub = 128, channels // 128
    count, wide = lax.axis_size(CTX), lax.axis_size("chan")
    tile = lambda *lead: jax.ShapeDtypeStruct((*lead, sub, lanes), F32)
    flat = lambda *dims: jax.ShapeDtypeStruct(dims, F32)
    rows = pltpu.VMEM((poles * sub, lanes), F32)
    parts = jnp.transpose(features, (1, 0, 2))
    edge = lax.ppermute(parts[:, toks - 2 :], CTX, [(i, i + 1) for i in range(count - 1)])
    state, product, query, consts = call(
        first_pass, "aaaa", (tile(poles), tile(toks), tile(toks), tile(poles + 16)),
        [
            pltpu.SMEM(contig_lengths.shape, jnp.int32),
            pltpu.VMEM((PIECES, 3, toks // PIECES, channels), jnp.bfloat16),
            pltpu.VMEM((3, sub * (toks + PAD), lanes), F32),
            pltpu.VMEM(short_taps.shape, F32),
            pltpu.VMEM(decay_rate.shape, F32),
            rows,
            pltpu.VMEM((9, sub, lanes), F32),
            pltpu.SemaphoreType.DMA((3,)),
            pltpu.SemaphoreType.DMA((PIECES,)),
        ],
        "first_pass",
    )(*[pltpu.with_memory_space_constraint(a, pltpu.HBM) for a in (contig_lengths, parts, short_taps, decay_rate)])
    ends, head = call(
        functools.partial(edge_pass, toks), "svvv", (tile(poles), tile(4)),
        [pltpu.VMEM((3, sub * 2, lanes), F32)], "edge_pass",
    )(contig_lengths, edge, consts, state)
    ends = lax.all_to_all(ends, ("row", "near"), 0, 0, tiled=True)
    totals = call(
        functools.partial(block_totals, toks), "svv",
        tile(lax.axis_size("row") * lax.axis_size("far")), [], "block_totals",
    )(contig_lengths, ends, consts)
    totals = lax.all_to_all(totals, "far", 0, 0, tiled=True)
    arrived = call(
        functools.partial(spread_carry, toks), "svvv", tile(poles), [], "spread_carry"
    )(contig_lengths, ends, totals, consts)
    arrived = lax.all_to_all(arrived, ("row", "near"), 0, 0, tiled=True)
    response, squares = call(
        second_pass, "svvvvvvv", (flat(toks, channels), flat(wide * toks // lanes, lanes)),
        [pltpu.VMEM((sub * toks, lanes), F32), pltpu.VMEM((poles, sub, lanes), F32), rows],
        "second_pass",
    )(contig_lengths, arrived, head, product, query, consts, residue,
      jnp.reshape(skip_gain, (sub, lanes)))
    squares = lax.all_to_all(squares, "chan", 0, 0, tiled=True)
    return call(
        last_pass, "vvv", jax.ShapeDtypeStruct((toks, channels), jnp.bfloat16), [], "last_pass"
    )(squares, response, jnp.reshape(norm_gain, (1, channels)))


def solution(mesh):
    chan = mesh.shape["chan"]
    inner = Mesh(mesh.devices.reshape(4, -1, 4, chan), CTX + ("chan",))
    placed = (
        P(CTX, None, "chan"),
        P(None, None, "chan"),
        P(None, "chan"),
        P(None, "chan"),
        P("chan"),
        P("chan"),
        P(),
    )
    return jax.shard_map(
        shards, mesh=inner, in_specs=placed, out_specs=P(CTX, "chan"), check_vma=False
    )
```

```python
import functools

import jax
import jax.numpy as jnp
from jax import lax
from jax.experimental import pallas as pl
from jax.experimental.pallas import tpu as pltpu
from jax.sharding import Mesh, PartitionSpec as P

D = 8192
eps_norm = 1e-05
CHUNK = 32
PAD = 8
PIECES = 2
CTX = ("row", "far", "near")
HIGH = lax.Precision.HIGHEST


def starts_of(lengths, anchor):
    one = lengths[0]
    two = one + lengths[1]
    three = two + lengths[2]
    return [-anchor, one - anchor, two - anchor, three - anchor]


def hits(starts, low, high):
    found = (starts[0] >= low) & (starts[0] < high)
    for start in starts[1:]:
        found = found | ((start >= low) & (start < high))
    return found


def as_tiles(rows, ref, sub, lanes):
    for tile in range(sub):
        rows[pl.ds(tile * ref.shape[0], ref.shape[0]), :] = ref[:, tile * lanes : (tile + 1) * lanes]


def row_tile(rows, row, count, sub):
    return rows[pl.ds(row, sub, stride=count), :]


def is_early():
    return lax.axis_index("far") < lax.axis_size("far") // 4


def mix(taps, now, one, two):
    return [taps[part] * now[part] + taps[3 + part] * one[part] + taps[6 + part] * two[part] for part in range(3)]


def scaled(rows, link):
    return [row * link for row in rows]


def link_at(starts, low, high):
    return jnp.where(hits(starts, low, high), 0.0, 1.0).astype(jnp.float32)


def first_pass(lengths_hbm, x_hbm, taps_hbm, rate_hbm, state_ref, product_ref, query_ref, consts_ref,
               lengths, held, spread, taps_held, rate_held, rate_rows, taps_rows, sems, x_sems):
    toks, sub, lanes = product_ref.shape
    poles = rate_held.shape[0]
    pitch = toks + PAD
    pieces = held.shape[0]
    span = toks // pieces
    small = [
        pltpu.make_async_copy(source, target, sems.at[i])
        for i, (source, target) in enumerate(
            [(lengths_hbm, lengths), (taps_hbm, taps_held), (rate_hbm, rate_held)]
        )
    ]
    for copy in small:
        copy.start()

    def piece_copy(piece):
        return pltpu.make_async_copy(
            x_hbm.at[:, pl.ds(pl.multiple_of(piece * span, span), span), :], held.at[piece], x_sems.at[piece]
        )

    for piece in range(pieces):
        piece_copy(piece).start()
    for copy in small:
        copy.wait()
    anchor = lax.axis_index(CTX) * toks
    starts = starts_of(lengths, anchor)
    as_tiles(rate_rows, rate_held, sub, lanes)
    for tap in range(3):
        for part in range(3):
            for tile in range(sub):
                taps_rows[tap * 3 + part, pl.ds(tile, 1), :] = taps_held[
                    tap, pl.ds(part, 1), tile * lanes : (tile + 1) * lanes
                ]
    fades = []
    for n in range(poles):
        rate = row_tile(rate_rows, n, poles, sub)
        consts_ref[n] = rate
        fades.append(jnp.exp(-rate))
    for row in range(9):
        consts_ref[poles + row] = taps_rows[row]
    state_ref[...] = jnp.zeros_like(state_ref)

    def token_rows(t):
        return [spread[part, pl.ds(t + PAD, sub, stride=pitch), :] for part in range(3)]

    def chunk(index, _):
        base = index * CHUNK

        def steps(masked):
            states = [state_ref[n] for n in range(poles)]
            two, one = token_rows(base - 2), token_rows(base - 1)
            for i in range(CHUNK):
                t = base + i
                now = token_rows(t)
                if masked:
                    link = link_at(starts, t, t + 1)
                    mixed = mix(taps_rows, now, scaled(one, link), scaled(two, link_at(starts, t - 1, t + 1)))
                    states = scaled(states, link)
                else:
                    mixed = mix(taps_rows, now, one, two)
                product = mixed[1] * mixed[2]
                query_ref[t] = mixed[0]
                product_ref[t] = product
                if masked and i < 2:
                    product = jnp.where(index == 0, 0.0, product)
                states = [fades[n] * states[n] + product for n in range(poles)]
                two, one = one, now
            for n in range(poles):
                state_ref[n] = states[n]

        cut = hits(starts, base - 1, base + CHUNK) | (index == 0)

        @pl.when(cut)
        def _():
            steps(True)

        @pl.when(jnp.logical_not(cut))
        def _():
            steps(False)

        return 0

    def piece_step(piece, _):
        piece_copy(piece).wait()
        for part in range(3):
            for tile in range(sub):
                row = pl.multiple_of(piece * span, span) + (tile * pitch + PAD)
                spread[part, pl.ds(pl.multiple_of(row, 8), span), :] = held[
                    piece, part, :, tile * lanes : (tile + 1) * lanes
                ].astype(jnp.float32)
        lax.fori_loop(piece * (span // CHUNK), (piece + 1) * (span // CHUNK), chunk, 0)
        return 0

    lax.fori_loop(0, pieces, piece_step, 0)
    for i in range(2):
        for part, row in enumerate(token_rows(i)):
            consts_ref[poles + 9 + i * 3 + part] = row


def edge_pass(lengths, edge_ref, consts_ref, state_ref, product_ref, residue_ref, skip_ref,
              ends_ref, head_ref, local_ref, gains_ref, spread, states_ref, residue_rows):
    toks = product_ref.shape[0]
    poles, sub, lanes = state_ref.shape
    anchor = lax.axis_index(CTX) * toks
    starts = starts_of(lengths, anchor)
    for part in range(3):
        for tile in range(sub):
            spread[part, pl.ds(tile * 2, 2), :] = edge_ref[
                part, :, tile * lanes : (tile + 1) * lanes
            ].astype(jnp.float32)
    earlier = [[spread[part, pl.ds(i, sub, stride=2), :] for part in range(3)] for i in range(2)]
    heads = [[consts_ref[poles + 9 + i * 3 + part] for part in range(3)] for i in range(2)]
    taps = [consts_ref[poles + row] for row in range(9)]
    at_zero = mix(taps, heads[0], scaled(earlier[1], link_at(starts, 0, 1)), scaled(earlier[0], link_at(starts, -1, 1)))
    at_one = mix(taps, heads[1], scaled(heads[0], link_at(starts, 1, 2)), scaled(earlier[1], link_at(starts, 0, 2)))
    zero, one = at_zero[1] * at_zero[2], at_one[1] * at_one[2]
    head_ref[0], head_ref[1], head_ref[2], head_ref[3] = zero, one, at_zero[0], at_one[0]
    zero, one = zero * link_at(starts, 1, toks), one * link_at(starts, 2, toks)
    for n in range(poles):
        rate = consts_ref[n]
        late = jnp.exp(rate * (-float(toks - 2)))
        ends_ref[n] = state_ref[n] + late * (jnp.exp(-rate) * zero + one)

    @pl.when(is_early())
    def _():
        fades, gains = fades_and_gains(consts_ref, residue_ref, residue_rows, sub, lanes)
        for n in range(poles):
            gains_ref[n] = gains[n]
        states_ref[...] = jnp.zeros_like(states_ref)

        def emit(t, _, product, total):
            local_ref[t] = total

        recurrence(starts, fades, gains, skip_ref[...], head_ref, product_ref, None, states_ref, emit)


def whole(starts, first, count):
    return link_at(starts, first, first + count)


def block_totals(toks, lengths, ends_ref, consts_ref, totals_ref):
    rows, near = lax.axis_size("row"), lax.axis_size("near")
    far = lax.axis_size("far")
    keep = jnp.exp(consts_ref[lax.axis_index("row") * near + lax.axis_index("near")] * (-float(toks)))
    starts = starts_of(lengths, 0)
    for row in range(rows):
        first = (row * far + lax.axis_index("far")) * (near * toks)
        total = ends_ref[row * near]
        for i in range(1, near):
            total = ends_ref[row * near + i] + total * (keep * whole(starts, first + i * toks, toks))
        for g in range(far):
            totals_ref[g * rows + row] = total


def spread_carry(toks, lengths, ends_ref, totals_ref, consts_ref, arrived_ref):
    rows, near, far = lax.axis_size("row"), lax.axis_size("near"), lax.axis_size("far")
    mine = lax.axis_index("far")
    rate = consts_ref[lax.axis_index("row") * near + lax.axis_index("near")]
    span = near * toks
    keep, keep_span = jnp.exp(rate * (-float(toks))), jnp.exp(rate * (-float(span)))
    starts = starts_of(lengths, 0)
    carry = jnp.zeros_like(keep)
    for row in range(rows):
        mid = carry
        for g in range(far):
            mid = jnp.where(g == mine, carry, mid)
            carry = totals_ref[g * rows + row] + carry * (keep_span * whole(starts, (row * far + g) * span, span))
        first = (row * far + mine) * span
        for i in range(near):
            arrived_ref[row * near + i] = mid
            mid = ends_ref[row * near + i] + mid * (keep * whole(starts, first + i * toks, toks))


def fades_and_gains(consts_ref, residue_ref, residue_rows, sub, lanes):
    as_tiles(residue_rows, residue_ref, sub, lanes)
    fades, gains = [], []
    for n in range(residue_ref.shape[0]):
        rate = consts_ref[n]
        fades.append(jnp.exp(-rate))
        gains.append(
            row_tile(residue_rows, n, residue_ref.shape[0], sub) * jnp.sqrt(1.0 - jnp.exp(-2.0 * rate))
        )
    return fades, gains


def summed(terms):
    while len(terms) > 1:
        terms = [a + b for a, b in zip(terms[::2], terms[1::2])] + ([terms[-1]] if len(terms) % 2 else [])
    return terms[0]


def recurrence(starts, fades, gains, skip, head_ref, product_ref, query_ref, states_ref, emit):
    poles = len(fades)

    def chunk(index, _):
        base = index * CHUNK

        def steps(masked):
            states = [states_ref[n] for n in range(poles)]
            for i in range(CHUNK):
                t = base + i
                product = product_ref[t]
                query = None if query_ref is None else query_ref[t]
                if masked:
                    states = scaled(states, link_at(starts, t, t + 1))
                    if i < 2:
                        product = jnp.where(index == 0, head_ref[i], product)
                        if query is not None:
                            query = jnp.where(index == 0, head_ref[2 + i], query)
                states = [fades[n] * states[n] + product for n in range(poles)]
                emit(t, query, product, summed([gains[n] * states[n] for n in range(poles)] + [skip * product]))
            for n in range(poles):
                states_ref[n] = states[n]

        cut = hits(starts, base, base + CHUNK) | (index == 0)

        @pl.when(cut)
        def _():
            steps(True)

        @pl.when(jnp.logical_not(cut))
        def _():
            steps(False)

        return 0

    lax.fori_loop(0, product_ref.shape[0] // CHUNK, chunk, 0)


def second_pass(lengths, arrived_ref, head_ref, local_ref, gains_ref, product_ref, query_ref, consts_ref,
                residue_ref, skip_ref, response_ref, squares_ref, spread, states_ref, residue_rows):
    toks, sub, lanes = product_ref.shape
    poles = residue_ref.shape[0]
    starts = starts_of(lengths, lax.axis_index(CTX) * toks)

    @pl.when(is_early())
    def _():
        fades = [jnp.exp(-consts_ref[n]) for n in range(poles)]
        for n in range(poles):
            states_ref[n] = arrived_ref[n] * gains_ref[n]

        def chunk(index, _):
            base = index * CHUNK

            def steps(masked):
                states = [states_ref[n] for n in range(poles)]
                for i in range(CHUNK):
                    t = base + i
                    query = query_ref[t]
                    states = [fades[n] * states[n] for n in range(poles)]
                    incoming = summed(list(states))
                    if masked:
                        incoming = incoming * link_at(starts, 0, t + 1)
                        if i < 2:
                            query = jnp.where(index == 0, head_ref[2 + i], query)
                    spread[pl.ds(t, sub, stride=toks), :] = query * (local_ref[t] + incoming)
                for n in range(poles):
                    states_ref[n] = states[n]

            cut = hits(starts, 0, base + CHUNK) | (index == 0)

            @pl.when(cut)
            def _():
                steps(True)

            @pl.when(jnp.logical_not(cut))
            def _():
                steps(False)

            return 0

        lax.fori_loop(0, toks // CHUNK, chunk, 0)

    @pl.when(jnp.logical_not(is_early()))
    def _():
        fades, gains = fades_and_gains(consts_ref, residue_ref, residue_rows, sub, lanes)
        states_ref[...] = arrived_ref[...]

        def emit(t, query, _, total):
            spread[pl.ds(t, sub, stride=toks), :] = query * total

        recurrence(starts, fades, gains, skip_ref[...], head_ref, product_ref, query_ref, states_ref, emit)

    total = jnp.zeros((toks, lanes), jnp.float32)
    for tile in range(sub):
        part = spread[pl.ds(tile * toks, toks), :]
        response_ref[:, tile * lanes : (tile + 1) * lanes] = part
        total = total + part * part
    sums = lax.dot_general(
        jnp.ones((squares_ref.shape[0], lanes), jnp.float32), total, (((1,), (1,)), ((), ())),
        precision=HIGH, preferred_element_type=jnp.float32,
    )
    halves = toks // lanes
    half = lax.broadcasted_iota(jnp.int32, squares_ref.shape, 0) % halves
    picked = sums[:, :lanes]
    for h in range(1, halves):
        picked = jnp.where(half == h, sums[:, h * lanes : (h + 1) * lanes], picked)
    squares_ref[...] = picked


def last_pass(squares_ref, response_ref, gain_ref, out_ref):
    count, lanes = squares_ref.shape
    halves = out_ref.shape[0] // lanes
    half = lax.broadcasted_iota(jnp.int32, (count, lanes), 0) % halves
    for h in range(halves):
        sums = lax.dot_general(
            squares_ref[...], (half == h).astype(jnp.float32), (((0,), (0,)), ((), ())),
            precision=HIGH, preferred_element_type=jnp.float32,
        )
        scale = lax.rsqrt(sums / D + eps_norm)
        toks = slice(h * lanes, (h + 1) * lanes)
        for tile in range(response_ref.shape[1] // lanes):
            cols = slice(tile * lanes, (tile + 1) * lanes)
            out_ref[toks, cols] = (response_ref[toks, cols] * scale * gain_ref[:, cols]).astype(jnp.bfloat16)


SCALARS = pl.BlockSpec(memory_space=pltpu.SMEM)
VECTORS = pl.BlockSpec(memory_space=pltpu.VMEM)
ANYWHERE = pl.BlockSpec(memory_space=pltpu.HBM)
F32 = jnp.float32
SPECS = {"s": SCALARS, "v": VECTORS, "a": ANYWHERE}


def call(body, inputs, outputs, scratch, name):
    return pl.pallas_call(
        body,
        in_specs=[SPECS[i] for i in inputs],
        out_specs=jax.tree.map(lambda _: VECTORS, outputs),
        out_shape=outputs,
        scratch_shapes=scratch,
        compiler_params=pltpu.CompilerParams(vmem_limit_bytes=40 << 20),
        name=name,
    )


def shards(features, short_taps, decay_rate, residue, skip_gain, norm_gain, contig_lengths):
    toks, _, channels = features.shape
    poles = decay_rate.shape[0]
    lanes, sub = 128, channels // 128
    count, wide = lax.axis_size(CTX), lax.axis_size("chan")
    tile = lambda *lead: jax.ShapeDtypeStruct((*lead, sub, lanes), F32)
    flat = lambda *dims: jax.ShapeDtypeStruct(dims, F32)
    rows = pltpu.VMEM((poles * sub, lanes), F32)
    parts = jnp.transpose(features, (1, 0, 2))
    edge = lax.ppermute(parts[:, toks - 2 :], CTX, [(i, i + 1) for i in range(count - 1)])
    state, product, query, consts = call(
        first_pass, "aaaa", (tile(poles), tile(toks), tile(toks), tile(poles + 16)),
        [
            pltpu.SMEM(contig_lengths.shape, jnp.int32),
            pltpu.VMEM((PIECES, 3, toks // PIECES, channels), jnp.bfloat16),
            pltpu.VMEM((3, sub * (toks + PAD), lanes), F32),
            pltpu.VMEM(short_taps.shape, F32),
            pltpu.VMEM(decay_rate.shape, F32),
            rows,
            pltpu.VMEM((9, sub, lanes), F32),
            pltpu.SemaphoreType.DMA((3,)),
            pltpu.SemaphoreType.DMA((PIECES,)),
        ],
        "first_pass",
    )(*[pltpu.with_memory_space_constraint(a, pltpu.HBM) for a in (contig_lengths, parts, short_taps, decay_rate)])
    states = pltpu.VMEM((poles, sub, lanes), F32)
    skip = jnp.reshape(skip_gain, (sub, lanes))
    ends, head, local, gains = call(
        edge_pass, "svvvvvv", (tile(poles), tile(4), tile(toks), tile(poles)),
        [pltpu.VMEM((3, sub * 2, lanes), F32), states, rows], "edge_pass",
    )(contig_lengths, edge, consts, state, product, residue, skip)
    ends = lax.all_to_all(ends, ("row", "near"), 0, 0, tiled=True)
    totals = call(
        functools.partial(block_totals, toks), "svv",
        tile(lax.axis_size("row") * lax.axis_size("far")), [], "block_totals",
    )(contig_lengths, ends, consts)
    totals = lax.all_to_all(totals, "far", 0, 0, tiled=True)
    arrived = call(
        functools.partial(spread_carry, toks), "svvv", tile(poles), [], "spread_carry"
    )(contig_lengths, ends, totals, consts)
    arrived = lax.all_to_all(arrived, ("row", "near"), 0, 0, tiled=True)
    response, squares = call(
        second_pass, "svvvvvvvvv", (flat(toks, channels), flat(wide * toks // lanes, lanes)),
        [pltpu.VMEM((sub * toks, lanes), F32), states, rows], "second_pass",
    )(contig_lengths, arrived, head, local, gains, product, query, consts, residue, skip)
    squares = lax.all_to_all(squares, "chan", 0, 0, tiled=True)
    return call(
        last_pass, "vvv", jax.ShapeDtypeStruct((toks, channels), jnp.bfloat16), [], "last_pass"
    )(squares, response, jnp.reshape(norm_gain, (1, channels)))


def solution(mesh):
    chan = mesh.shape["chan"]
    inner = Mesh(mesh.devices.reshape(4, -1, 4, chan), CTX + ("chan",))
    placed = (
        P(CTX, None, "chan"),
        P(None, None, "chan"),
        P(None, "chan"),
        P(None, "chan"),
        P("chan"),
        P("chan"),
        P(),
    )
    return jax.shard_map(
        shards, mesh=inner, in_specs=placed, out_specs=P(CTX, "chan"), check_vma=False
    )
```

```python
import functools

import jax
import jax.numpy as jnp
from jax import lax
from jax.experimental import pallas as pl
from jax.experimental.pallas import tpu as pltpu
from jax.sharding import Mesh, PartitionSpec as P

D = 8192
eps_norm = 1e-05
CHUNK = 32
PAD = 8
PIECES = 2
CTX = ("row", "far", "near")
HIGH = lax.Precision.HIGHEST


def starts_of(lengths, anchor):
    one = lengths[0]
    two = one + lengths[1]
    three = two + lengths[2]
    return [-anchor, one - anchor, two - anchor, three - anchor]


def hits(starts, low, high):
    found = (starts[0] >= low) & (starts[0] < high)
    for start in starts[1:]:
        found = found | ((start >= low) & (start < high))
    return found


def marked(marks_ref, anchor):
    return [marks_ref[k] - anchor for k in range(marks_ref.shape[0])]


def marked_scalars(marks_ref, anchor):
    return [
        jnp.max(marks_ref[k].astype(jnp.float32)).astype(jnp.int32) - anchor for k in range(marks_ref.shape[0])
    ]


def as_tiles(rows, ref, sub, lanes):
    for tile in range(sub):
        rows[pl.ds(tile * ref.shape[0], ref.shape[0]), :] = ref[:, tile * lanes : (tile + 1) * lanes]


def row_tile(rows, row, count, sub):
    return rows[pl.ds(row, sub, stride=count), :]


def is_early():
    return lax.axis_index("far") < lax.axis_size("far") // 4


def mix(taps, now, one, two):
    return [taps[part] * now[part] + taps[3 + part] * one[part] + taps[6 + part] * two[part] for part in range(3)]


def scaled(rows, link):
    return [row * link for row in rows]


def link_at(starts, low, high):
    return jnp.where(hits(starts, low, high), 0.0, 1.0).astype(jnp.float32)


def first_pass(lengths_hbm, x_hbm, taps_hbm, rate_hbm, state_ref, product_ref, query_ref, consts_ref, marks_ref,
               lengths, held, spread, taps_held, rate_held, rate_rows, taps_rows, sems, x_sems):
    toks, sub, lanes = product_ref.shape
    poles = rate_held.shape[0]
    pitch = toks + PAD
    pieces = held.shape[0]
    span = toks // pieces
    small = [
        pltpu.make_async_copy(source, target, sems.at[i])
        for i, (source, target) in enumerate(
            [(lengths_hbm, lengths), (taps_hbm, taps_held), (rate_hbm, rate_held)]
        )
    ]
    for copy in small:
        copy.start()

    def piece_copy(piece):
        return pltpu.make_async_copy(
            x_hbm.at[:, pl.ds(pl.multiple_of(piece * span, span), span), :], held.at[piece], x_sems.at[piece]
        )

    for piece in range(pieces):
        piece_copy(piece).start()
    for copy in small:
        copy.wait()
    anchor = lax.axis_index(CTX) * toks
    starts = starts_of(lengths, anchor)
    for k, start in enumerate(starts_of(lengths, 0)):
        marks_ref[k] = jnp.full((sub, lanes), start, jnp.int32)
    as_tiles(rate_rows, rate_held, sub, lanes)
    for tap in range(3):
        for part in range(3):
            for tile in range(sub):
                taps_rows[tap * 3 + part, pl.ds(tile, 1), :] = taps_held[
                    tap, pl.ds(part, 1), tile * lanes : (tile + 1) * lanes
                ]
    fades = []
    for n in range(poles):
        rate = row_tile(rate_rows, n, poles, sub)
        consts_ref[n] = rate
        fades.append(jnp.exp(-rate))
    for row in range(9):
        consts_ref[poles + row] = taps_rows[row]
    state_ref[...] = jnp.zeros_like(state_ref)

    def token_rows(t):
        return [spread[part, pl.ds(t + PAD, sub, stride=pitch), :] for part in range(3)]

    def chunk(index, _):
        base = index * CHUNK

        def steps(masked):
            states = [state_ref[n] for n in range(poles)]
            two, one = token_rows(base - 2), token_rows(base - 1)
            for i in range(CHUNK):
                t = base + i
                now = token_rows(t)
                if masked:
                    link = link_at(starts, t, t + 1)
                    mixed = mix(taps_rows, now, scaled(one, link), scaled(two, link_at(starts, t - 1, t + 1)))
                    states = scaled(states, link)
                else:
                    mixed = mix(taps_rows, now, one, two)
                product = mixed[1] * mixed[2]
                query_ref[t] = mixed[0]
                product_ref[t] = product
                if masked and i < 2:
                    product = jnp.where(index == 0, 0.0, product)
                states = [fades[n] * states[n] + product for n in range(poles)]
                two, one = one, now
            for n in range(poles):
                state_ref[n] = states[n]

        cut = hits(starts, base - 1, base + CHUNK) | (index == 0)

        @pl.when(cut)
        def _():
            steps(True)

        @pl.when(jnp.logical_not(cut))
        def _():
            steps(False)

        return 0

    def piece_step(piece, _):
        piece_copy(piece).wait()
        for part in range(3):
            for tile in range(sub):
                row = pl.multiple_of(piece * span, span) + (tile * pitch + PAD)
                spread[part, pl.ds(pl.multiple_of(row, 8), span), :] = held[
                    piece, part, :, tile * lanes : (tile + 1) * lanes
                ].astype(jnp.float32)
        lax.fori_loop(piece * (span // CHUNK), (piece + 1) * (span // CHUNK), chunk, 0)
        return 0

    lax.fori_loop(0, pieces, piece_step, 0)
    for i in range(2):
        for part, row in enumerate(token_rows(i)):
            consts_ref[poles + 9 + i * 3 + part] = row


def edge_pass(marks_ref, edge_ref, consts_ref, state_ref, product_ref, residue_ref, skip_ref,
              ends_ref, head_ref, local_ref, gains_ref, spread, states_ref, residue_rows):
    toks = product_ref.shape[0]
    poles, sub, lanes = state_ref.shape
    anchor = lax.axis_index(CTX) * toks
    starts = marked(marks_ref, anchor)
    for part in range(3):
        for tile in range(sub):
            spread[part, pl.ds(tile * 2, 2), :] = edge_ref[
                part, :, tile * lanes : (tile + 1) * lanes
            ].astype(jnp.float32)
    earlier = [[spread[part, pl.ds(i, sub, stride=2), :] for part in range(3)] for i in range(2)]
    heads = [[consts_ref[poles + 9 + i * 3 + part] for part in range(3)] for i in range(2)]
    taps = [consts_ref[poles + row] for row in range(9)]
    at_zero = mix(taps, heads[0], scaled(earlier[1], link_at(starts, 0, 1)), scaled(earlier[0], link_at(starts, -1, 1)))
    at_one = mix(taps, heads[1], scaled(heads[0], link_at(starts, 1, 2)), scaled(earlier[1], link_at(starts, 0, 2)))
    zero, one = at_zero[1] * at_zero[2], at_one[1] * at_one[2]
    head_ref[0], head_ref[1], head_ref[2], head_ref[3] = zero, one, at_zero[0], at_one[0]
    zero, one = zero * link_at(starts, 1, toks), one * link_at(starts, 2, toks)
    for n in range(poles):
        rate = consts_ref[n]
        late = jnp.exp(rate * (-float(toks - 2)))
        ends_ref[n] = state_ref[n] + late * (jnp.exp(-rate) * zero + one)

    @pl.when(is_early())
    def _():
        fades, gains = fades_and_gains(consts_ref, residue_ref, residue_rows, sub, lanes)
        for n in range(poles):
            gains_ref[n] = gains[n]
        states_ref[...] = jnp.zeros_like(states_ref)

        def emit(t, _, product, total):
            local_ref[t] = total

        recurrence(marked_scalars(marks_ref, anchor), fades, gains, skip_ref[...], head_ref, product_ref, None, states_ref, emit)


def whole(starts, first, count):
    return link_at(starts, first, first + count)


def block_totals(toks, marks_ref, ends_ref, consts_ref, totals_ref):
    rows, near = lax.axis_size("row"), lax.axis_size("near")
    far = lax.axis_size("far")
    keep = jnp.exp(consts_ref[lax.axis_index("row") * near + lax.axis_index("near")] * (-float(toks)))
    starts = marked(marks_ref, 0)
    for row in range(rows):
        first = (row * far + lax.axis_index("far")) * (near * toks)
        total = ends_ref[row * near]
        for i in range(1, near):
            total = ends_ref[row * near + i] + total * (keep * whole(starts, first + i * toks, toks))
        for g in range(far):
            totals_ref[g * rows + row] = total


def spread_carry(toks, marks_ref, ends_ref, totals_ref, consts_ref, arrived_ref):
    rows, near, far = lax.axis_size("row"), lax.axis_size("near"), lax.axis_size("far")
    mine = lax.axis_index("far")
    rate = consts_ref[lax.axis_index("row") * near + lax.axis_index("near")]
    span = near * toks
    keep, keep_span = jnp.exp(rate * (-float(toks))), jnp.exp(rate * (-float(span)))
    starts = marked(marks_ref, 0)
    carry = jnp.zeros_like(keep)
    for row in range(rows):
        mid = carry
        for g in range(far):
            mid = jnp.where(g == mine, carry, mid)
            carry = totals_ref[g * rows + row] + carry * (keep_span * whole(starts, (row * far + g) * span, span))
        first = (row * far + mine) * span
        for i in range(near):
            arrived_ref[row * near + i] = mid
            mid = ends_ref[row * near + i] + mid * (keep * whole(starts, first + i * toks, toks))


def fades_and_gains(consts_ref, residue_ref, residue_rows, sub, lanes):
    as_tiles(residue_rows, residue_ref, sub, lanes)
    fades, gains = [], []
    for n in range(residue_ref.shape[0]):
        rate = consts_ref[n]
        fades.append(jnp.exp(-rate))
        gains.append(
            row_tile(residue_rows, n, residue_ref.shape[0], sub) * jnp.sqrt(1.0 - jnp.exp(-2.0 * rate))
        )
    return fades, gains


def summed(terms):
    while len(terms) > 1:
        terms = [a + b for a, b in zip(terms[::2], terms[1::2])] + ([terms[-1]] if len(terms) % 2 else [])
    return terms[0]


def recurrence(starts, fades, gains, skip, head_ref, product_ref, query_ref, states_ref, emit):
    poles = len(fades)

    def chunk(index, _):
        base = index * CHUNK

        def steps(masked):
            states = [states_ref[n] for n in range(poles)]
            for i in range(CHUNK):
                t = base + i
                product = product_ref[t]
                query = None if query_ref is None else query_ref[t]
                if masked:
                    states = scaled(states, link_at(starts, t, t + 1))
                    if i < 2:
                        product = jnp.where(index == 0, head_ref[i], product)
                        if query is not None:
                            query = jnp.where(index == 0, head_ref[2 + i], query)
                states = [fades[n] * states[n] + product for n in range(poles)]
                emit(t, query, product, summed([gains[n] * states[n] for n in range(poles)] + [skip * product]))
            for n in range(poles):
                states_ref[n] = states[n]

        cut = hits(starts, base, base + CHUNK) | (index == 0)

        @pl.when(cut)
        def _():
            steps(True)

        @pl.when(jnp.logical_not(cut))
        def _():
            steps(False)

        return 0

    lax.fori_loop(0, product_ref.shape[0] // CHUNK, chunk, 0)


def second_pass(marks_ref, arrived_ref, head_ref, local_ref, gains_ref, product_ref, query_ref, consts_ref,
                residue_ref, skip_ref, response_ref, squares_ref, spread, states_ref, residue_rows):
    toks, sub, lanes = product_ref.shape
    poles = residue_ref.shape[0]
    starts = marked_scalars(marks_ref, lax.axis_index(CTX) * toks)

    @pl.when(is_early())
    def _():
        fades = [jnp.exp(-consts_ref[n]) for n in range(poles)]
        for n in range(poles):
            states_ref[n] = arrived_ref[n] * gains_ref[n]

        def chunk(index, _):
            base = index * CHUNK

            def steps(masked):
                states = [states_ref[n] for n in range(poles)]
                for i in range(CHUNK):
                    t = base + i
                    query = query_ref[t]
                    states = [fades[n] * states[n] for n in range(poles)]
                    incoming = summed(list(states))
                    if masked:
                        incoming = incoming * link_at(starts, 0, t + 1)
                        if i < 2:
                            query = jnp.where(index == 0, head_ref[2 + i], query)
                    spread[pl.ds(t, sub, stride=toks), :] = query * (local_ref[t] + incoming)
                for n in range(poles):
                    states_ref[n] = states[n]

            cut = hits(starts, 0, base + CHUNK) | (index == 0)

            @pl.when(cut)
            def _():
                steps(True)

            @pl.when(jnp.logical_not(cut))
            def _():
                steps(False)

            return 0

        lax.fori_loop(0, toks // CHUNK, chunk, 0)

    @pl.when(jnp.logical_not(is_early()))
    def _():
        fades, gains = fades_and_gains(consts_ref, residue_ref, residue_rows, sub, lanes)
        states_ref[...] = arrived_ref[...]

        def emit(t, query, _, total):
            spread[pl.ds(t, sub, stride=toks), :] = query * total

        recurrence(starts, fades, gains, skip_ref[...], head_ref, product_ref, query_ref, states_ref, emit)

    total = jnp.zeros((toks, lanes), jnp.float32)
    for tile in range(sub):
        part = spread[pl.ds(tile * toks, toks), :]
        response_ref[:, tile * lanes : (tile + 1) * lanes] = part
        total = total + part * part
    sums = lax.dot_general(
        jnp.ones((squares_ref.shape[0], lanes), jnp.float32), total, (((1,), (1,)), ((), ())),
        precision=HIGH, preferred_element_type=jnp.float32,
    )
    halves = toks // lanes
    half = lax.broadcasted_iota(jnp.int32, squares_ref.shape, 0) % halves
    picked = sums[:, :lanes]
    for h in range(1, halves):
        picked = jnp.where(half == h, sums[:, h * lanes : (h + 1) * lanes], picked)
    squares_ref[...] = picked


def last_pass(squares_ref, response_ref, gain_ref, out_ref):
    count, lanes = squares_ref.shape
    halves = out_ref.shape[0] // lanes
    half = lax.broadcasted_iota(jnp.int32, (count, lanes), 0) % halves
    for h in range(halves):
        sums = lax.dot_general(
            squares_ref[...], (half == h).astype(jnp.float32), (((0,), (0,)), ((), ())),
            precision=HIGH, preferred_element_type=jnp.float32,
        )
        scale = lax.rsqrt(sums / D + eps_norm)
        toks = slice(h * lanes, (h + 1) * lanes)
        for tile in range(response_ref.shape[1] // lanes):
            cols = slice(tile * lanes, (tile + 1) * lanes)
            out_ref[toks, cols] = (response_ref[toks, cols] * scale * gain_ref[:, cols]).astype(jnp.bfloat16)


SCALARS = pl.BlockSpec(memory_space=pltpu.SMEM)
VECTORS = pl.BlockSpec(memory_space=pltpu.VMEM)
ANYWHERE = pl.BlockSpec(memory_space=pltpu.HBM)
F32 = jnp.float32
SPECS = {"s": SCALARS, "v": VECTORS, "a": ANYWHERE}


def call(body, inputs, outputs, scratch, name):
    return pl.pallas_call(
        body,
        in_specs=[SPECS[i] for i in inputs],
        out_specs=jax.tree.map(lambda _: VECTORS, outputs),
        out_shape=outputs,
        scratch_shapes=scratch,
        compiler_params=pltpu.CompilerParams(vmem_limit_bytes=40 << 20),
        name=name,
    )


def shards(features, short_taps, decay_rate, residue, skip_gain, norm_gain, contig_lengths):
    toks, _, channels = features.shape
    poles = decay_rate.shape[0]
    lanes, sub = 128, channels // 128
    count, wide = lax.axis_size(CTX), lax.axis_size("chan")
    tile = lambda *lead: jax.ShapeDtypeStruct((*lead, sub, lanes), F32)
    flat = lambda *dims: jax.ShapeDtypeStruct(dims, F32)
    rows = pltpu.VMEM((poles * sub, lanes), F32)
    parts = jnp.transpose(features, (1, 0, 2))
    edge = lax.ppermute(parts[:, toks - 2 :], CTX, [(i, i + 1) for i in range(count - 1)])
    marks_shape = jax.ShapeDtypeStruct((contig_lengths.shape[0], sub, lanes), jnp.int32)
    state, product, query, consts, marks = call(
        first_pass, "aaaa", (tile(poles), tile(toks), tile(toks), tile(poles + 16), marks_shape),
        [
            pltpu.SMEM(contig_lengths.shape, jnp.int32),
            pltpu.VMEM((PIECES, 3, toks // PIECES, channels), jnp.bfloat16),
            pltpu.VMEM((3, sub * (toks + PAD), lanes), F32),
            pltpu.VMEM(short_taps.shape, F32),
            pltpu.VMEM(decay_rate.shape, F32),
            rows,
            pltpu.VMEM((9, sub, lanes), F32),
            pltpu.SemaphoreType.DMA((3,)),
            pltpu.SemaphoreType.DMA((PIECES,)),
        ],
        "first_pass",
    )(*[pltpu.with_memory_space_constraint(a, pltpu.HBM) for a in (contig_lengths, parts, short_taps, decay_rate)])
    states = pltpu.VMEM((poles, sub, lanes), F32)
    skip = jnp.reshape(skip_gain, (sub, lanes))
    ends, head, local, gains = call(
        edge_pass, "vvvvvvv", (tile(poles), tile(4), tile(toks), tile(poles)),
        [pltpu.VMEM((3, sub * 2, lanes), F32), states, rows], "edge_pass",
    )(marks, edge, consts, state, product, residue, skip)
    ends = lax.all_to_all(ends, ("row", "near"), 0, 0, tiled=True)
    totals = call(
        functools.partial(block_totals, toks), "vvv",
        tile(lax.axis_size("row") * lax.axis_size("far")), [], "block_totals",
    )(marks, ends, consts)
    totals = lax.all_to_all(totals, "far", 0, 0, tiled=True)
    arrived = call(
        functools.partial(spread_carry, toks), "vvvv", tile(poles), [], "spread_carry"
    )(marks, ends, totals, consts)
    arrived = lax.all_to_all(arrived, ("row", "near"), 0, 0, tiled=True)
    response, squares = call(
        second_pass, "vvvvvvvvvv", (flat(toks, channels), flat(wide * toks // lanes, lanes)),
        [pltpu.VMEM((sub * toks, lanes), F32), states, rows], "second_pass",
    )(marks, arrived, head, local, gains, product, query, consts, residue, skip)
    squares = lax.all_to_all(squares, "chan", 0, 0, tiled=True)
    return call(
        last_pass, "vvv", jax.ShapeDtypeStruct((toks, channels), jnp.bfloat16), [], "last_pass"
    )(squares, response, jnp.reshape(norm_gain, (1, channels)))


def solution(mesh):
    chan = mesh.shape["chan"]
    inner = Mesh(mesh.devices.reshape(4, -1, 4, chan), CTX + ("chan",))
    placed = (
        P(CTX, None, "chan"),
        P(None, None, "chan"),
        P(None, "chan"),
        P(None, "chan"),
        P("chan"),
        P("chan"),
        P(),
    )
    return jax.shard_map(
        shards, mesh=inner, in_specs=placed, out_specs=P(CTX, "chan"), check_vma=False
    )
```

```python
import functools

import jax
import jax.numpy as jnp
from jax import lax
from jax.experimental import pallas as pl
from jax.experimental.pallas import tpu as pltpu
from jax.sharding import Mesh, PartitionSpec as P

D = 8192
eps_norm = 1e-05
CHUNK = 32
PAD = 8
PIECES = 2
CTX = ("row", "far", "near")


def starts_of(lengths, anchor):
    one = lengths[0]
    two = one + lengths[1]
    three = two + lengths[2]
    return [-anchor, one - anchor, two - anchor, three - anchor]


def hits(starts, low, high):
    found = (starts[0] >= low) & (starts[0] < high)
    for start in starts[1:]:
        found = found | ((start >= low) & (start < high))
    return found


def marked(marks_ref, anchor):
    return [marks_ref[k] - anchor for k in range(marks_ref.shape[0])]


def marked_scalars(marks_ref, anchor):
    return [
        jnp.max(marks_ref[k].astype(jnp.float32)).astype(jnp.int32) - anchor for k in range(marks_ref.shape[0])
    ]


def as_tiles(rows, ref, sub, lanes):
    for tile in range(sub):
        rows[pl.ds(tile * ref.shape[0], ref.shape[0]), :] = ref[:, tile * lanes : (tile + 1) * lanes]


def row_tile(rows, row, count, sub):
    return rows[pl.ds(row, sub, stride=count), :]


def is_early():
    return lax.axis_index("far") < lax.axis_size("far") // 4


def mix(taps, now, one, two):
    return [taps[part] * now[part] + taps[3 + part] * one[part] + taps[6 + part] * two[part] for part in range(3)]


def scaled(rows, link):
    return [row * link for row in rows]


def link_at(starts, low, high):
    return jnp.where(hits(starts, low, high), 0.0, 1.0).astype(jnp.float32)


def first_pass(lengths_hbm, x_hbm, taps_hbm, rate_hbm, state_ref, product_ref, query_ref, consts_ref, marks_ref,
               lengths, held, spread, taps_held, rate_held, rate_rows, taps_rows, sems, x_sems):
    toks, sub, lanes = product_ref.shape
    poles = rate_held.shape[0]
    pitch = toks + PAD
    pieces = held.shape[0]
    span = toks // pieces
    small = [
        pltpu.make_async_copy(source, target, sems.at[i])
        for i, (source, target) in enumerate(
            [(lengths_hbm, lengths), (taps_hbm, taps_held), (rate_hbm, rate_held)]
        )
    ]
    for copy in small:
        copy.start()

    def piece_copy(piece):
        return pltpu.make_async_copy(
            x_hbm.at[:, pl.ds(pl.multiple_of(piece * span, span), span), :], held.at[piece], x_sems.at[piece]
        )

    for piece in range(pieces):
        piece_copy(piece).start()
    for copy in small:
        copy.wait()
    anchor = lax.axis_index(CTX) * toks
    starts = starts_of(lengths, anchor)
    for k, start in enumerate(starts_of(lengths, 0)):
        marks_ref[k] = jnp.full((sub, lanes), start, jnp.int32)
    as_tiles(rate_rows, rate_held, sub, lanes)
    for tap in range(3):
        for part in range(3):
            for tile in range(sub):
                taps_rows[tap * 3 + part, pl.ds(tile, 1), :] = taps_held[
                    tap, pl.ds(part, 1), tile * lanes : (tile + 1) * lanes
                ]
    fades = []
    for n in range(poles):
        rate = row_tile(rate_rows, n, poles, sub)
        consts_ref[n] = rate
        fades.append(jnp.exp(-rate))
    for row in range(9):
        consts_ref[poles + row] = taps_rows[row]
    state_ref[...] = jnp.zeros_like(state_ref)

    def token_rows(t):
        return [spread[part, pl.ds(t + PAD, sub, stride=pitch), :] for part in range(3)]

    def chunk(index, _):
        base = index * CHUNK

        def steps(masked):
            states = [state_ref[n] for n in range(poles)]
            two, one = token_rows(base - 2), token_rows(base - 1)
            for i in range(CHUNK):
                t = base + i
                now = token_rows(t)
                if masked:
                    link = link_at(starts, t, t + 1)
                    mixed = mix(taps_rows, now, scaled(one, link), scaled(two, link_at(starts, t - 1, t + 1)))
                    states = scaled(states, link)
                else:
                    mixed = mix(taps_rows, now, one, two)
                product = mixed[1] * mixed[2]
                query_ref[t] = mixed[0]
                product_ref[t] = product
                if masked and i < 2:
                    product = jnp.where(index == 0, 0.0, product)
                states = [fades[n] * states[n] + product for n in range(poles)]
                two, one = one, now
            for n in range(poles):
                state_ref[n] = states[n]

        cut = hits(starts, base - 1, base + CHUNK) | (index == 0)

        @pl.when(cut)
        def _():
            steps(True)

        @pl.when(jnp.logical_not(cut))
        def _():
            steps(False)

        return 0

    def piece_step(piece, _):
        piece_copy(piece).wait()
        for part in range(3):
            for tile in range(sub):
                row = pl.multiple_of(piece * span, span) + (tile * pitch + PAD)
                spread[part, pl.ds(pl.multiple_of(row, 8), span), :] = held[
                    piece, part, :, tile * lanes : (tile + 1) * lanes
                ].astype(jnp.float32)
        lax.fori_loop(piece * (span // CHUNK), (piece + 1) * (span // CHUNK), chunk, 0)
        return 0

    lax.fori_loop(0, pieces, piece_step, 0)
    for i in range(2):
        for part, row in enumerate(token_rows(i)):
            consts_ref[poles + 9 + i * 3 + part] = row


def edge_pass(marks_ref, edge_ref, consts_ref, state_ref, product_ref, residue_ref, skip_ref,
              ends_ref, head_ref, local_ref, gains_ref, spread, states_ref, residue_rows):
    toks = product_ref.shape[0]
    poles, sub, lanes = state_ref.shape
    anchor = lax.axis_index(CTX) * toks
    starts = marked(marks_ref, anchor)
    for part in range(3):
        for tile in range(sub):
            spread[part, pl.ds(tile * 2, 2), :] = edge_ref[
                part, :, tile * lanes : (tile + 1) * lanes
            ].astype(jnp.float32)
    earlier = [[spread[part, pl.ds(i, sub, stride=2), :] for part in range(3)] for i in range(2)]
    heads = [[consts_ref[poles + 9 + i * 3 + part] for part in range(3)] for i in range(2)]
    taps = [consts_ref[poles + row] for row in range(9)]
    at_zero = mix(taps, heads[0], scaled(earlier[1], link_at(starts, 0, 1)), scaled(earlier[0], link_at(starts, -1, 1)))
    at_one = mix(taps, heads[1], scaled(heads[0], link_at(starts, 1, 2)), scaled(earlier[1], link_at(starts, 0, 2)))
    zero, one = at_zero[1] * at_zero[2], at_one[1] * at_one[2]
    head_ref[0], head_ref[1], head_ref[2], head_ref[3] = zero, one, at_zero[0], at_one[0]
    zero, one = zero * link_at(starts, 1, toks), one * link_at(starts, 2, toks)
    for n in range(poles):
        rate = consts_ref[n]
        late = jnp.exp(rate * (-float(toks - 2)))
        ends_ref[n] = state_ref[n] + late * (jnp.exp(-rate) * zero + one)

    @pl.when(is_early())
    def _():
        fades, gains = fades_and_gains(consts_ref, residue_ref, residue_rows, sub, lanes)
        for n in range(poles):
            gains_ref[n] = gains[n]
        states_ref[...] = jnp.zeros_like(states_ref)

        def emit(t, _, product, total):
            local_ref[t] = total

        recurrence(marked_scalars(marks_ref, anchor), fades, gains, skip_ref[...], head_ref, product_ref, None, states_ref, emit)


def whole(starts, first, count):
    return link_at(starts, first, first + count)


def block_totals(toks, marks_ref, ends_ref, consts_ref, totals_ref):
    rows, near = lax.axis_size("row"), lax.axis_size("near")
    far = lax.axis_size("far")
    keep = jnp.exp(consts_ref[lax.axis_index("row") * near + lax.axis_index("near")] * (-float(toks)))
    starts = marked(marks_ref, 0)
    for row in range(rows):
        first = (row * far + lax.axis_index("far")) * (near * toks)
        total = ends_ref[row * near]
        for i in range(1, near):
            total = ends_ref[row * near + i] + total * (keep * whole(starts, first + i * toks, toks))
        for g in range(far):
            totals_ref[g * rows + row] = total


def spread_carry(toks, marks_ref, ends_ref, totals_ref, consts_ref, arrived_ref):
    rows, near, far = lax.axis_size("row"), lax.axis_size("near"), lax.axis_size("far")
    mine = lax.axis_index("far")
    rate = consts_ref[lax.axis_index("row") * near + lax.axis_index("near")]
    span = near * toks
    keep, keep_span = jnp.exp(rate * (-float(toks))), jnp.exp(rate * (-float(span)))
    starts = marked(marks_ref, 0)
    carry = jnp.zeros_like(keep)
    for row in range(rows):
        mid = carry
        for g in range(far):
            mid = jnp.where(g == mine, carry, mid)
            carry = totals_ref[g * rows + row] + carry * (keep_span * whole(starts, (row * far + g) * span, span))
        first = (row * far + mine) * span
        for i in range(near):
            arrived_ref[row * near + i] = mid
            mid = ends_ref[row * near + i] + mid * (keep * whole(starts, first + i * toks, toks))


def fades_and_gains(consts_ref, residue_ref, residue_rows, sub, lanes):
    as_tiles(residue_rows, residue_ref, sub, lanes)
    fades, gains = [], []
    for n in range(residue_ref.shape[0]):
        rate = consts_ref[n]
        fades.append(jnp.exp(-rate))
        gains.append(
            row_tile(residue_rows, n, residue_ref.shape[0], sub) * jnp.sqrt(1.0 - jnp.exp(-2.0 * rate))
        )
    return fades, gains


def summed(terms):
    while len(terms) > 1:
        terms = [a + b for a, b in zip(terms[::2], terms[1::2])] + ([terms[-1]] if len(terms) % 2 else [])
    return terms[0]


def recurrence(starts, fades, gains, skip, head_ref, product_ref, query_ref, states_ref, emit):
    poles = len(fades)

    def chunk(index, _):
        base = index * CHUNK

        def steps(masked):
            states = [states_ref[n] for n in range(poles)]
            for i in range(CHUNK):
                t = base + i
                product = product_ref[t]
                query = None if query_ref is None else query_ref[t]
                if masked:
                    states = scaled(states, link_at(starts, t, t + 1))
                    if i < 2:
                        product = jnp.where(index == 0, head_ref[i], product)
                        if query is not None:
                            query = jnp.where(index == 0, head_ref[2 + i], query)
                states = [fades[n] * states[n] + product for n in range(poles)]
                emit(t, query, product, summed([gains[n] * states[n] for n in range(poles)] + [skip * product]))
            for n in range(poles):
                states_ref[n] = states[n]

        cut = hits(starts, base, base + CHUNK) | (index == 0)

        @pl.when(cut)
        def _():
            steps(True)

        @pl.when(jnp.logical_not(cut))
        def _():
            steps(False)

        return 0

    lax.fori_loop(0, product_ref.shape[0] // CHUNK, chunk, 0)


def in_thirds(value, axis):
    high = value.astype(jnp.bfloat16)
    rest = value - high.astype(jnp.float32)
    middle = rest.astype(jnp.bfloat16)
    low = (rest - middle.astype(jnp.float32)).astype(jnp.bfloat16)
    return jnp.concatenate([high, middle, low], axis)


def second_pass(marks_ref, arrived_ref, head_ref, local_ref, gains_ref, product_ref, query_ref, consts_ref,
                residue_ref, skip_ref, response_ref, squares_ref, spread, states_ref, residue_rows):
    toks, sub, lanes = product_ref.shape
    poles = residue_ref.shape[0]
    starts = marked_scalars(marks_ref, lax.axis_index(CTX) * toks)

    @pl.when(is_early())
    def _():
        fades = [jnp.exp(-consts_ref[n]) for n in range(poles)]
        for n in range(poles):
            states_ref[n] = arrived_ref[n] * gains_ref[n]

        def chunk(index, _):
            base = index * CHUNK

            def steps(masked):
                states = [states_ref[n] for n in range(poles)]
                for i in range(CHUNK):
                    t = base + i
                    query = query_ref[t]
                    states = [fades[n] * states[n] for n in range(poles)]
                    incoming = summed(list(states))
                    if masked:
                        incoming = incoming * link_at(starts, 0, t + 1)
                        if i < 2:
                            query = jnp.where(index == 0, head_ref[2 + i], query)
                    spread[pl.ds(t, sub, stride=toks), :] = query * (local_ref[t] + incoming)
                for n in range(poles):
                    states_ref[n] = states[n]

            cut = hits(starts, 0, base + CHUNK) | (index == 0)

            @pl.when(cut)
            def _():
                steps(True)

            @pl.when(jnp.logical_not(cut))
            def _():
                steps(False)

            return 0

        lax.fori_loop(0, toks // CHUNK, chunk, 0)

    @pl.when(jnp.logical_not(is_early()))
    def _():
        fades, gains = fades_and_gains(consts_ref, residue_ref, residue_rows, sub, lanes)
        states_ref[...] = arrived_ref[...]

        def emit(t, query, _, total):
            spread[pl.ds(t, sub, stride=toks), :] = query * total

        recurrence(starts, fades, gains, skip_ref[...], head_ref, product_ref, query_ref, states_ref, emit)

    total = jnp.zeros((toks, lanes), jnp.float32)
    for tile in range(sub):
        part = spread[pl.ds(tile * toks, toks), :]
        response_ref[:, tile * lanes : (tile + 1) * lanes] = part
        total = total + part * part
    sums = lax.dot_general(
        jnp.ones((squares_ref.shape[0], 3 * lanes), jnp.bfloat16), in_thirds(total, 1), (((1,), (1,)), ((), ())),
        preferred_element_type=jnp.float32,
    )
    halves = toks // lanes
    half = lax.broadcasted_iota(jnp.int32, squares_ref.shape, 0) % halves
    picked = sums[:, :lanes]
    for h in range(1, halves):
        picked = jnp.where(half == h, sums[:, h * lanes : (h + 1) * lanes], picked)
    squares_ref[...] = picked


def last_pass(squares_ref, response_ref, gain_ref, out_ref):
    count, lanes = squares_ref.shape
    halves = out_ref.shape[0] // lanes
    half = lax.broadcasted_iota(jnp.int32, (3 * count, lanes), 0) % halves
    parts = in_thirds(squares_ref[...], 0)
    for h in range(halves):
        sums = lax.dot_general(
            parts, (half == h).astype(jnp.bfloat16), (((0,), (0,)), ((), ())),
            preferred_element_type=jnp.float32,
        )
        scale = lax.rsqrt(sums / D + eps_norm)
        toks = slice(h * lanes, (h + 1) * lanes)
        for tile in range(response_ref.shape[1] // lanes):
            cols = slice(tile * lanes, (tile + 1) * lanes)
            out_ref[toks, cols] = (response_ref[toks, cols] * scale * gain_ref[:, cols]).astype(jnp.bfloat16)


SCALARS = pl.BlockSpec(memory_space=pltpu.SMEM)
VECTORS = pl.BlockSpec(memory_space=pltpu.VMEM)
ANYWHERE = pl.BlockSpec(memory_space=pltpu.HBM)
F32 = jnp.float32
SPECS = {"s": SCALARS, "v": VECTORS, "a": ANYWHERE}


def call(body, inputs, outputs, scratch, name):
    return pl.pallas_call(
        body,
        in_specs=[SPECS[i] for i in inputs],
        out_specs=jax.tree.map(lambda _: VECTORS, outputs),
        out_shape=outputs,
        scratch_shapes=scratch,
        compiler_params=pltpu.CompilerParams(vmem_limit_bytes=40 << 20),
        name=name,
    )


def shards(features, short_taps, decay_rate, residue, skip_gain, norm_gain, contig_lengths):
    toks, _, channels = features.shape
    poles = decay_rate.shape[0]
    lanes, sub = 128, channels // 128
    count, wide = lax.axis_size(CTX), lax.axis_size("chan")
    tile = lambda *lead: jax.ShapeDtypeStruct((*lead, sub, lanes), F32)
    flat = lambda *dims: jax.ShapeDtypeStruct(dims, F32)
    rows = pltpu.VMEM((poles * sub, lanes), F32)
    parts = jnp.transpose(features, (1, 0, 2))
    edge = lax.ppermute(parts[:, toks - 2 :], CTX, [(i, i + 1) for i in range(count - 1)])
    marks_shape = jax.ShapeDtypeStruct((contig_lengths.shape[0], sub, lanes), jnp.int32)
    state, product, query, consts, marks = call(
        first_pass, "aaaa", (tile(poles), tile(toks), tile(toks), tile(poles + 16), marks_shape),
        [
            pltpu.SMEM(contig_lengths.shape, jnp.int32),
            pltpu.VMEM((PIECES, 3, toks // PIECES, channels), jnp.bfloat16),
            pltpu.VMEM((3, sub * (toks + PAD), lanes), F32),
            pltpu.VMEM(short_taps.shape, F32),
            pltpu.VMEM(decay_rate.shape, F32),
            rows,
            pltpu.VMEM((9, sub, lanes), F32),
            pltpu.SemaphoreType.DMA((3,)),
            pltpu.SemaphoreType.DMA((PIECES,)),
        ],
        "first_pass",
    )(*[pltpu.with_memory_space_constraint(a, pltpu.HBM) for a in (contig_lengths, parts, short_taps, decay_rate)])
    states = pltpu.VMEM((poles, sub, lanes), F32)
    skip = jnp.reshape(skip_gain, (sub, lanes))
    ends, head, local, gains = call(
        edge_pass, "vvvvvvv", (tile(poles), tile(4), tile(toks), tile(poles)),
        [pltpu.VMEM((3, sub * 2, lanes), F32), states, rows], "edge_pass",
    )(marks, edge, consts, state, product, residue, skip)
    ends = lax.all_to_all(ends, ("row", "near"), 0, 0, tiled=True)
    totals = call(
        functools.partial(block_totals, toks), "vvv",
        tile(lax.axis_size("row") * lax.axis_size("far")), [], "block_totals",
    )(marks, ends, consts)
    totals = lax.all_to_all(totals, "far", 0, 0, tiled=True)
    arrived = call(
        functools.partial(spread_carry, toks), "vvvv", tile(poles), [], "spread_carry"
    )(marks, ends, totals, consts)
    arrived = lax.all_to_all(arrived, ("row", "near"), 0, 0, tiled=True)
    response, squares = call(
        second_pass, "vvvvvvvvvv", (flat(toks, channels), flat(wide * toks // lanes, lanes)),
        [pltpu.VMEM((sub * toks, lanes), F32), states, rows], "second_pass",
    )(marks, arrived, head, local, gains, product, query, consts, residue, skip)
    squares = lax.all_to_all(squares, "chan", 0, 0, tiled=True)
    return call(
        last_pass, "vvv", jax.ShapeDtypeStruct((toks, channels), jnp.bfloat16), [], "last_pass"
    )(squares, response, jnp.reshape(norm_gain, (1, channels)))


def solution(mesh):
    chan = mesh.shape["chan"]
    inner = Mesh(mesh.devices.reshape(4, -1, 4, chan), CTX + ("chan",))
    placed = (
        P(CTX, None, "chan"),
        P(None, None, "chan"),
        P(None, "chan"),
        P(None, "chan"),
        P("chan"),
        P("chan"),
        P(),
    )
    return jax.shard_map(
        shards, mesh=inner, in_specs=placed, out_specs=P(CTX, "chan"), check_vma=False
    )
```
